32 devices in a mesh: grp: 2 (over y), stn: 8 (over z, x), tim: 2 (over core).
Axes of the slice: x: 2, y: 2, z: 4, core: 2. Of those that a mesh axis runs over, the one named last changes fastest.
Arguments:
- samples: bfloat16 [256, 32, 8192], P(('grp', 'stn'), 'tim'), parts along dimension 0, may hold values from -6 to 6
- taps: float32 [16, 8192], replicated, may hold values from -1.5 to 1.5
- flags: int32 [256, 32], P('grp'), parts along dimension 0, may hold values from 0 to 1, as said below
- group_owner: int32 [16], P('grp'), parts along dimension 0, may hold values from 0 to 7, each once
Outputs:
- visibility: float32 [16, 128, 2, 128], P(('grp', 'stn'), 'tim'), parts along dimension 0
The draws below stay inside these ranges and needn't reach their ends.
There are 2 independent parts, one for each index of `grp`. The reference program is written for one: setup_inputs(seed, part) draws one part's arguments, and reference() takes and returns one part's arrays. A program takes and returns all parts, laid end to end along the dimension named above; an argument that names none is the same for every part. Nothing has to cross between parts.
Inputs may be any that keep to these rules, and one draw needn't show every extreme that they name: `flags`: each channel's 1 entries form one circular run of consecutive frames, of length 0 to 32. `group_owner`: a permutation of the channel groups.
All inputs are finite; a program needn't handle non-finite values.
Results may differ from the reference program's by a relative error of at most 0.0063.
Values may be sent and summed in bfloat16 or wider, within the bound.
A program may use at most 320 MiB of HBM per device.

```python
import math
import jax
import jax.numpy as jnp
from jax import lax

INPUTS = 128
FFT = 8192
TAPS = 16
AVG = 16
BAND = 128
BAND_START = 1536
FRAMES = 32
N_STN = 8


def draw_flags(key, part):
    count_key, start_key = jax.random.split(jax.random.fold_in(key, 17))
    run_length = jax.random.randint(count_key, (BAND, 1), 0, FRAMES + 1)
    run_start = jax.random.randint(start_key, (BAND, 1), 0, FRAMES)
    positions = jnp.arange(FRAMES, dtype=jnp.int32)[None, :]
    return ((positions - run_start) % FRAMES < run_length).astype(jnp.int32)


def shard_levels(key, shape, cuts, least, top_value):
    loudness = 1.0
    for position, shards_of in cuts:
        steps = jax.random.uniform(jax.random.fold_in(jax.random.fold_in(key, 6), position), (shards_of,), jnp.float32, least / len(cuts), top_value / len(cuts))
        loudness = loudness * jnp.repeat(jnp.exp(steps), shape[position] // shards_of).reshape((-1,) + (1,) * (len(shape) - 1 - position))
    return loudness


def scatter_about(rng, dims, width, most, cuts=(), held_as=jnp.bfloat16):
    drawn = jax.random.normal(rng, dims, jnp.float32) * width
    if len(cuts) > 0:
        drawn = shard_levels(rng, dims, cuts, -0.22, 0.18) * drawn
    return jnp.clip(drawn, min=-most, max=most).astype(held_as)


def setup_inputs(seed: int = 0, part: int = 0) -> dict:
    key_of = jax.random.split(jax.random.key(seed), 5)
    own_keys = jax.random.split(jax.random.fold_in(key_of[4], part), 5)
    return {
        "samples": scatter_about(own_keys[0], (INPUTS, FRAMES, FFT), 1.0, 6.0, ((0, 8), (1, 2))),
        "taps": scatter_about(key_of[1], (TAPS, FFT), TAPS ** -0.5, 1.5, (), jnp.float32),
        "flags": draw_flags(jax.random.fold_in(jax.random.fold_in(key_of[4], part), 71), part),
        "group_owner": jax.random.permutation(own_keys[3], N_STN).astype(jnp.int32),
    }


def build_table(fft_len, channel_ids):
    positions = jnp.arange(fft_len, dtype=jnp.int32)
    phase_index = positions[:, None] * (BAND_START + channel_ids)[None, :] % fft_len
    angle = phase_index.astype(jnp.float32) * (2.0 * math.pi / fft_len)
    amplitude = 1.0 / math.sqrt(fft_len)
    real_part = jnp.cos(angle) * amplitude
    imag_part = -jnp.sin(angle) * amplitude
    return jnp.stack([real_part, imag_part], axis=-1).astype(jnp.bfloat16)

def reference(samples, taps, flags, group_owner):
    inputs, frames, fft_len = samples.shape
    band_width = flags.shape[0]
    group_total = band_width // AVG
    twiddle = build_table(fft_len, jnp.arange(band_width, dtype=jnp.int32)).astype(jnp.float32).reshape(fft_len, 2 * band_width)
    block_size = math.gcd(inputs, 64)

    def channelize(block_samples):
        padded = jnp.concatenate([jnp.zeros((block_size, TAPS - 1, fft_len), samples.dtype), block_samples], axis=1)
        filtered = jnp.zeros((block_size, frames, fft_len), jnp.float32)
        for tap_index in range(TAPS):
            filtered = filtered + taps[tap_index][None, None, :] * padded[:, tap_index:tap_index + frames, :].astype(jnp.float32)
        rounded = lax.optimization_barrier(filtered.astype(jnp.bfloat16))
        frame_rows = rounded.astype(jnp.float32).reshape(block_size * frames, fft_len)
        spectrum = jnp.dot(frame_rows, twiddle, precision=lax.Precision.HIGHEST).astype(jnp.bfloat16)
        return spectrum.reshape(block_size, frames, band_width, 2)
    spectra = lax.map(channelize, samples.reshape(inputs // block_size, block_size, frames, fft_len))
    spectra = spectra.reshape(inputs, frames, band_width, 2)
    weighted = spectra * flags.T.astype(jnp.bfloat16)[None, :, :, None]

    def correlate(group_id):
        sliced = lax.dynamic_slice_in_dim(weighted, group_id * AVG, AVG, axis=2).astype(jnp.float32)
        left_rows = sliced.reshape(inputs, -1)
        turned = jnp.stack([sliced[..., 1], -sliced[..., 0]], axis=-1).reshape(inputs, -1)
        real_part = jnp.dot(left_rows, left_rows.T, precision=lax.Precision.HIGHEST)
        imag_part = jnp.dot(turned, left_rows.T, precision=lax.Precision.HIGHEST)
        return jnp.stack([real_part, imag_part], axis=1) / (AVG * frames)
    owned_group = jnp.zeros((group_total,), jnp.int32).at[group_owner].set(jnp.arange(group_total, dtype=jnp.int32))
    return lax.map(correlate, owned_group)
```

```python
import functools
import math

import jax
import jax.numpy as jnp
import numpy as np
from jax import lax
from jax.experimental import pallas as pl
from jax.experimental.pallas import tpu as pltpu
from jax.sharding import PartitionSpec as P

BAND_START = 1536
MESH = pl.DeviceIdType.MESH
LANES = 128
ROW_BLOCK = 64


def phase_tables(fft_len, groups, per_group):
    channels = np.arange(groups * per_group).reshape(groups, per_group) + BAND_START

    def planes(first, second):
        stacked = np.stack([first, second], axis=-2)
        return stacked.reshape(stacked.shape[0], -1).astype(np.float32)

    def angle(positions):
        index = (positions[:, None, None].astype(np.int64) * channels[None]) % fft_len
        return index * (2.0 * math.pi / fft_len)

    outer = angle(np.arange(fft_len // LANES) * LANES)
    inner = angle(np.arange(LANES))
    amplitude = 1.0 / math.sqrt(fft_len)
    outer_same = planes(np.cos(outer), np.cos(outer))
    outer_cross = planes(np.sin(outer), -np.sin(outer))
    inner_own = planes(np.cos(inner) * amplitude, -np.sin(inner) * amplitude)
    inner_swap = planes(-np.sin(inner) * amplitude, np.cos(inner) * amplitude)
    return outer_same, outer_cross, inner_own, inner_swap


def spectra_kernel(samples_ref, taps_ref, same_ref, cross_ref, own_ref, swap_ref, out_ref, wide, rows, table):
    inputs, frames, width = samples_ref.shape
    taps_count = taps_ref.shape[0]
    out_frames = frames + taps_count - 1
    step = pl.program_id(0)

    @pl.when(step == 0)
    def _():
        out_ref[...] = jnp.zeros_like(out_ref)
        rows[out_frames * inputs :, :] = jnp.zeros((rows.shape[0] - out_frames * inputs, width), rows.dtype)

    for chunk in range(width // LANES):
        lanes = slice(chunk * LANES, (chunk + 1) * LANES)
        slot = wide.at[chunk % 2]
        slot[...] = samples_ref[:, :, lanes].astype(jnp.float32).reshape(inputs * frames, LANES)
        weights = [
            jnp.broadcast_to(taps_ref[k : k + 1, lanes], (inputs, LANES)).astype(FILTER_TYPE)
            for k in range(taps_count)
        ]
        frame = [slot[pl.ds(s, inputs, stride=frames), :].astype(FILTER_TYPE) for s in range(frames)]
        for t in range(out_frames):
            terms = []
            for k in range(taps_count):
                s = t - (taps_count - 1) + k
                if 0 <= s < frames:
                    terms.append(weights[k] * frame[s])
            while len(terms) > 1:
                paired = [terms[m] + terms[m + 1] for m in range(0, len(terms) - 1, 2)]
                terms = paired + (terms[-1:] if len(terms) % 2 else [])
            rows[t * inputs : (t + 1) * inputs, lanes] = terms[0].astype(rows.dtype)
        table[lanes, :] = (
            same_ref[chunk : chunk + 1, :] * own_ref[...] + cross_ref[chunk : chunk + 1, :] * swap_ref[...]
        ).astype(table.dtype)
    out_ref[...] += jnp.dot(rows[...], table[...], preferred_element_type=jnp.float32)


FILTER_TYPE = jnp.float32


def partial_spectra(samples, taps, tables):
    inputs, frames, fft_len = samples.shape
    taps_count = taps.shape[0]
    columns = tables[0].shape[1]
    width = min(1024, fft_len)
    row_count = -(-(frames + taps_count - 1) * inputs // 128) * 128
    whole = lambda j: (0, 0)
    return pl.pallas_call(
        spectra_kernel,
        grid=(fft_len // width,),
        in_specs=[
            pl.BlockSpec((inputs, frames, width), lambda j: (0, 0, j)),
            pl.BlockSpec((taps_count, width), lambda j: (0, j)),
            pl.BlockSpec((width // LANES, columns), lambda j: (j, 0)),
            pl.BlockSpec((width // LANES, columns), lambda j: (j, 0)),
            pl.BlockSpec((LANES, columns), whole),
            pl.BlockSpec((LANES, columns), whole),
        ],
        out_specs=pl.BlockSpec((row_count, columns), whole),
        out_shape=jax.ShapeDtypeStruct((row_count, columns), jnp.float32),
        scratch_shapes=[
            pltpu.VMEM((2, inputs * frames, LANES), jnp.float32),
            pltpu.VMEM((row_count, width), jnp.bfloat16),
            pltpu.VMEM((width, columns), jnp.bfloat16),
        ],
        compiler_params=pltpu.CompilerParams(vmem_limit_bytes=48 << 20),
        name="filter_and_transform",
    )(samples, taps, *tables)


def correlate_kernel(
    dims, owner_ref, partial_ref, flags_ref, out_ref,
    earlier, spectra, outgoing, received, products, other,
    near_sem, send_sem, recv_sem, final_sem,
):
    stations, inputs, frames, per_group = dims
    me = lax.axis_index("stn")
    half = lax.axis_index("tim")
    wide = 2 * per_group
    columns = stations * wide
    own_rows = frames * inputs
    per_lane = LANES // wide

    barrier = pltpu.get_barrier_semaphore()
    pl.semaphore_signal(barrier, inc=1, device_id={"tim": 1 - half}, device_id_type=MESH)

    def greet(d, carry):
        pl.semaphore_signal(
            barrier, inc=1, device_id={"stn": lax.rem(me + d, stations)}, device_id_type=MESH
        )
        return carry

    lax.fori_loop(1, stations, greet, 0)

    band = stations * per_group
    channel = lax.broadcasted_iota(jnp.int32, (band, columns), 0)
    column = lax.broadcasted_iota(jnp.int32, (band, columns), 1)
    spread = (channel == column // wide * per_group + column % per_group).astype(jnp.bfloat16)
    flag_rows = flags_ref[...].astype(jnp.float32).astype(jnp.bfloat16)
    valid = jnp.dot(flag_rows, spread, preferred_element_type=jnp.float32)
    valid = jnp.where(half == 0, valid[:frames], valid[frames:])

    lane = lax.broadcasted_iota(jnp.int32, (8, columns), 1)
    target = lane % wide
    for g in range(stations):
        target = jnp.where(lane // wide == g, target + owner_ref[g] * wide, target)
    target = target[:1]

    pl.semaphore_wait(barrier, stations)

    carry_rows = earlier.shape[0]
    near = pltpu.make_async_remote_copy(
        src_ref=partial_ref.at[pl.ds(own_rows, carry_rows), :],
        dst_ref=earlier,
        send_sem=near_sem.at[0],
        recv_sem=near_sem.at[1],
        device_id={"tim": 1 - half},
        device_id_type=MESH,
    )

    @pl.when(half == 0)
    def _():
        near.start()
        spectra[...] = partial_ref[:own_rows, :].astype(jnp.bfloat16)

    @pl.when(half == 1)
    def _():
        near.wait_recv()
        spectra[:carry_rows, :] = (partial_ref[:carry_rows, :] + earlier[...]).astype(jnp.bfloat16)
        spectra[carry_rows:, :] = partial_ref[carry_rows:own_rows, :].astype(jnp.bfloat16)

    weighted = spectra[...].reshape(frames, inputs, columns) * valid.astype(jnp.bfloat16)[:, None, :]
    spectra[...] = weighted.reshape(own_rows, columns)

    slot = lax.broadcasted_iota(jnp.int32, (inputs, LANES), 1) // wide

    def arrange(b, carry):
        row = lax.broadcasted_iota(jnp.int32, (LANES, columns), 0) + b * LANES
        picked = (row == target).astype(jnp.bfloat16)
        block = lax.dot_general(
            spectra[...], picked, (((1,), (1,)), ((), ())), preferred_element_type=jnp.float32
        )
        for r in range(per_lane):
            for quad in range(frames // per_lane):
                total = jnp.zeros((inputs, LANES), jnp.float32)
                for t in range(per_lane):
                    first = (quad * per_lane + t) * inputs
                    piece = block[first : first + inputs, :]
                    if t != r:
                        piece = pltpu.roll(piece, ((t - r) * wide) % LANES, 1)
                    total = jnp.where(slot == t, piece, total)
                outgoing[b * per_lane + r, :, quad * LANES : (quad + 1) * LANES] = total.astype(jnp.bfloat16)
        return carry

    lax.fori_loop(0, stations // per_lane, arrange, 0)

    def turn_copy(d):
        to = lax.rem(me + d, stations)
        return pltpu.make_async_remote_copy(
            src_ref=outgoing.at[to],
            dst_ref=received.at[me],
            send_sem=send_sem.at[d],
            recv_sem=recv_sem.at[d],
            device_id={"stn": to},
            device_id_type=MESH,
        )

    def send(d, carry):
        turn_copy(d).start()
        return carry

    lax.fori_loop(1, stations, send, 0)
    received[me] = outgoing[me]

    def arrive(d, carry):
        turn_copy(d).wait_recv()
        return carry

    lax.fori_loop(1, stations, arrive, 0)

    total_inputs = stations * inputs
    length = frames * wide
    per_block = ROW_BLOCK // inputs
    plane = lax.broadcasted_iota(jnp.int32, (ROW_BLOCK, length), 1) // per_group % 2
    everything = received[...].reshape(total_inputs, length)

    def correlate(b, carry):
        left = received[pl.ds(b * per_block, per_block)].reshape(ROW_BLOCK, length)
        full = left.astype(jnp.float32)
        turned = jnp.where(
            plane == 0, pltpu.roll(full, length - per_group, 1), -pltpu.roll(full, per_group, 1)
        ).astype(jnp.bfloat16)
        both = jnp.concatenate([left, turned], axis=0)
        product = lax.dot_general(
            both, everything, (((1,), (1,)), ((), ())), preferred_element_type=jnp.float32
        )
        products[b] = product.reshape(2, ROW_BLOCK, total_inputs)
        return carry

    lax.fori_loop(0, total_inputs // ROW_BLOCK, correlate, 0)

    mine = out_ref.shape[0]
    last = pltpu.make_async_remote_copy(
        src_ref=products.at[pl.ds((1 - half) * mine, mine)],
        dst_ref=other,
        send_sem=final_sem.at[0],
        recv_sem=final_sem.at[1],
        device_id={"tim": 1 - half},
        device_id_type=MESH,
    )
    last.start()

    def sent(d, carry):
        turn_copy(d).wait_send()
        return carry

    lax.fori_loop(1, stations, sent, 0)

    @pl.when(half == 0)
    def _():
        near.wait_send()

    last.wait()
    normaliser = 1.0 / (per_group * frames * 2)
    out_ref[...] = (products[pl.ds(half * mine, mine)] + other[...]) * normaliser


def correlate(partial, flags, group_owner, stations, inputs, frames, per_group, carry_frames):
    columns = stations * 2 * per_group
    total_inputs = stations * inputs
    blocks = total_inputs // ROW_BLOCK
    length = frames * 2 * per_group
    vmem = pl.BlockSpec(memory_space=pltpu.VMEM)
    return pl.pallas_call(
        functools.partial(correlate_kernel, (stations, inputs, frames, per_group)),
        in_specs=[pl.BlockSpec(memory_space=pltpu.SMEM), vmem, vmem],
        out_specs=vmem,
        out_shape=jax.ShapeDtypeStruct((blocks // 2, 2, ROW_BLOCK, total_inputs), jnp.float32),
        scratch_shapes=[
            pltpu.VMEM((carry_frames * inputs, columns), jnp.float32),
            pltpu.VMEM((frames * inputs, columns), jnp.bfloat16),
            pltpu.VMEM((stations, inputs, length), jnp.bfloat16),
            pltpu.VMEM((stations, inputs, length), jnp.bfloat16),
            pltpu.VMEM((blocks, 2, ROW_BLOCK, total_inputs), jnp.float32),
            pltpu.VMEM((blocks // 2, 2, ROW_BLOCK, total_inputs), jnp.float32),
            pltpu.SemaphoreType.DMA((2,)),
            pltpu.SemaphoreType.DMA((stations,)),
            pltpu.SemaphoreType.DMA((stations,)),
            pltpu.SemaphoreType.DMA((2,)),
        ],
        compiler_params=pltpu.CompilerParams(
            collective_id=0, has_side_effects=True, vmem_limit_bytes=56 << 20
        ),
        name="turn_and_correlate",
    )(group_owner, partial, flags)


def per_device(samples, taps, flags, group_owner):
    inputs, frames, fft_len = samples.shape
    stations = lax.axis_size("stn")
    per_group = flags.shape[0] // stations
    tables = [jnp.asarray(t) for t in phase_tables(fft_len, stations, per_group)]
    partial = partial_spectra(samples, taps, tables)
    blocks = correlate(
        partial, flags.T, group_owner, stations, inputs, frames, per_group, taps.shape[0] - 1
    )
    return blocks.transpose(0, 2, 1, 3).reshape(1, -1, 2, stations * inputs)


def solution(mesh):
    in_specs = (P(("grp", "stn"), "tim", None), P(), P("grp", None), P("grp"))
    out_specs = P(("grp", "stn"), "tim", None, None)
    return jax.shard_map(
        per_device, mesh=mesh, in_specs=in_specs, out_specs=out_specs, check_vma=False
    )
```

```python
import functools
import math

import jax
import jax.numpy as jnp
import numpy as np
from jax import lax
from jax.experimental import pallas as pl
from jax.experimental.pallas import tpu as pltpu
from jax.sharding import PartitionSpec as P

BAND_START = 1536
MESH = pl.DeviceIdType.MESH
LANES = 128
ROW_BLOCK = 64
STEP_WIDTH = 1024
TABLE_LIMIT = 8 << 20


def phase_tables(fft_len, groups, per_group):
    channels = np.arange(groups * per_group).reshape(groups, per_group) + BAND_START

    def planes(first, second):
        stacked = np.stack([first, second], axis=-2)
        return stacked.reshape(stacked.shape[0], -1).astype(np.float32)

    def angle(positions):
        index = (positions[:, None, None].astype(np.int64) * channels[None]) % fft_len
        return index * (2.0 * math.pi / fft_len)

    outer = angle(np.arange(fft_len // LANES) * LANES)
    inner = angle(np.arange(LANES))
    amplitude = 1.0 / math.sqrt(fft_len)
    outer_same = planes(np.cos(outer), np.cos(outer))
    outer_cross = planes(np.sin(outer), -np.sin(outer))
    inner_own = planes(np.cos(inner) * amplitude, -np.sin(inner) * amplitude)
    inner_swap = planes(-np.sin(inner) * amplitude, np.cos(inner) * amplitude)
    return outer_same, outer_cross, inner_own, inner_swap


def filter_chunk(samples_ref, taps_ref, wide, rows, lanes, to):
    inputs, frames, _ = samples_ref.shape
    taps_count = taps_ref.shape[0]
    wide[...] = samples_ref[:, :, lanes].astype(jnp.float32).reshape(inputs * frames, LANES)
    weights = [
        jnp.broadcast_to(taps_ref[k : k + 1, lanes], (inputs, LANES)).astype(jnp.bfloat16)
        for k in range(taps_count)
    ]
    frame = [wide[pl.ds(s, inputs, stride=frames), :].astype(jnp.bfloat16) for s in range(frames)]
    for t in range(frames + taps_count - 1):
        first = t - (taps_count - 1)
        terms = [weights[k] * frame[first + k] for k in range(taps_count) if 0 <= first + k < frames]
        while len(terms) > 1:
            paired = [terms[m] + terms[m + 1] for m in range(0, len(terms) - 1, 2)]
            terms = paired + (terms[-1:] if len(terms) % 2 else [])
        rows[t * inputs : (t + 1) * inputs, to] = terms[0]


def kernel(
    dims, owner_ref, samples_ref, taps_ref, same_ref, cross_ref, own_ref, swap_ref, flags_ref, out_ref,
    wide, rows, table, total, valid, later, earlier, spectra, outgoing, received, products, other,
    near_sem, send_sem, recv_sem, final_sem,
):
    stations, per_group, steps, span = dims
    inputs, frames, width = samples_ref.shape
    carry_rows = later.shape[0]
    own_rows = frames * inputs
    group_width = 2 * per_group
    columns = stations * group_width
    per_lane = LANES // group_width
    step = pl.program_id(0)
    me = lax.axis_index("stn")
    half = lax.axis_index("tim")
    barrier = pltpu.get_barrier_semaphore()

    @pl.when(step == 0)
    def _():
        pl.semaphore_signal(barrier, inc=1, device_id={"tim": 1 - half}, device_id_type=MESH)

        def greet(d, carry):
            pl.semaphore_signal(
                barrier, inc=1, device_id={"stn": lax.rem(me + d, stations)}, device_id_type=MESH
            )
            return carry

        lax.fori_loop(1, stations, greet, 0)
        if span < steps:
            total[...] = jnp.zeros_like(total)
        band = stations * per_group
        channel = lax.broadcasted_iota(jnp.int32, (band, columns), 0)
        column = lax.broadcasted_iota(jnp.int32, (band, columns), 1)
        spread = (channel == column // group_width * per_group + column % per_group).astype(jnp.bfloat16)
        flag_rows = flags_ref[...].astype(jnp.float32).astype(jnp.bfloat16)
        both = jnp.dot(flag_rows, spread, preferred_element_type=jnp.float32)
        valid[...] = jnp.where(half == 0, both[:frames], both[frames:])

    place = lax.rem(step, span) * width

    def chunk(c, carry):
        lanes = pl.ds(pl.multiple_of(c * LANES, LANES), LANES)
        to = pl.ds(pl.multiple_of(place + c * LANES, LANES), LANES)
        filter_chunk(samples_ref, taps_ref, wide, rows, lanes, to)
        table[to, :] = (
            same_ref[pl.ds(c, 1), :] * own_ref[...] + cross_ref[pl.ds(c, 1), :] * swap_ref[...]
        ).astype(table.dtype)
        return carry

    lax.fori_loop(0, width // LANES, chunk, 0)

    def transform(low, high):
        return jnp.dot(rows[low:high, :], table[...], preferred_element_type=jnp.float32)

    if span < steps:

        @pl.when(jnp.logical_and(lax.rem(step, span) == span - 1, step < steps - 1))
        def _():
            total[...] += transform(0, own_rows + carry_rows)

    @pl.when(step == steps - 1)
    def _():
        def finished(low, high):
            result = transform(low, high)
            return result + total[low:high, :] if span < steps else result

        later[...] = finished(own_rows, own_rows + carry_rows)
        pl.semaphore_wait(barrier, stations)
        near = pltpu.make_async_remote_copy(
            src_ref=later,
            dst_ref=earlier,
            send_sem=near_sem.at[0],
            recv_sem=near_sem.at[1],
            device_id={"tim": 1 - half},
            device_id_type=MESH,
        )

        @pl.when(half == 0)
        def _():
            near.start()

        mine = finished(0, own_rows)
        lane = lax.broadcasted_iota(jnp.int32, (8, columns), 1)
        target = lane % group_width
        for g in range(stations):
            target = jnp.where(lane // group_width == g, target + owner_ref[g] * group_width, target)
        target = target[:1]
        mask = valid[...].astype(jnp.bfloat16)

        def weigh(values, low, high):
            count = high - low
            shaped = values.astype(jnp.bfloat16).reshape(count, inputs, columns)
            spectra[low * inputs : high * inputs, :] = (shaped * mask[low:high, None, :]).reshape(
                count * inputs, columns
            )

        @pl.when(half == 0)
        def _():
            weigh(mine, 0, frames)

        @pl.when(half == 1)
        def _():
            near.wait_recv()
            carried = carry_rows // inputs
            weigh(mine[:carry_rows] + earlier[...], 0, carried)
            weigh(mine[carry_rows:], carried, frames)

        slot = lax.broadcasted_iota(jnp.int32, (inputs, LANES), 1) // group_width

        def turn_copy(d):
            to = lax.rem(me + d, stations)
            return pltpu.make_async_remote_copy(
                src_ref=outgoing.at[to],
                dst_ref=received.at[me],
                send_sem=send_sem.at[d],
                recv_sem=recv_sem.at[d],
                device_id={"stn": to},
                device_id_type=MESH,
            )

        def arrange(b, carry):
            row = lax.broadcasted_iota(jnp.int32, (LANES, columns), 0) + b * LANES
            picked = (row == target).astype(jnp.bfloat16)
            block = lax.dot_general(
                spectra[...], picked, (((1,), (1,)), ((), ())), preferred_element_type=jnp.float32
            )
            for r in range(per_lane):
                for quad in range(frames // per_lane):
                    joined = jnp.zeros((inputs, LANES), jnp.float32)
                    for t in range(per_lane):
                        first = (quad * per_lane + t) * inputs
                        piece = block[first : first + inputs, :]
                        if t != r:
                            piece = pltpu.roll(piece, ((t - r) * group_width) % LANES, 1)
                        joined = jnp.where(slot == t, piece, joined)
                    outgoing[b * per_lane + r, :, quad * LANES : (quad + 1) * LANES] = joined.astype(
                        jnp.bfloat16
                    )
            return carry

        lax.fori_loop(0, stations // per_lane, arrange, 0)

        def send(d, carry):
            turn_copy(d).start()
            return carry

        lax.fori_loop(1, stations, send, 0)
        received[me] = outgoing[me]

        def arrive(d, carry):
            turn_copy(d).wait_recv()
            return carry

        lax.fori_loop(1, stations, arrive, 0)

        total_inputs = stations * inputs
        length = frames * group_width
        per_block = ROW_BLOCK // inputs
        plane = lax.broadcasted_iota(jnp.int32, (ROW_BLOCK, length), 1) // per_group % 2
        everything = received[...].reshape(total_inputs, length)

        def correlate(b, carry):
            left = received[pl.ds(b * per_block, per_block)].reshape(ROW_BLOCK, length)
            full = left.astype(jnp.float32)
            turned = jnp.where(
                plane == 0, pltpu.roll(full, length - per_group, 1), -pltpu.roll(full, per_group, 1)
            ).astype(jnp.bfloat16)
            pair = jnp.concatenate([left, turned], axis=0)
            product = lax.dot_general(
                pair, everything, (((1,), (1,)), ((), ())), preferred_element_type=jnp.float32
            )
            products[b] = product.reshape(2, ROW_BLOCK, total_inputs)
            return carry

        blocks = out_ref.shape[0]
        last = pltpu.make_async_remote_copy(
            src_ref=products.at[pl.ds((1 - half) * blocks, blocks)],
            dst_ref=other,
            send_sem=final_sem.at[0],
            recv_sem=final_sem.at[1],
            device_id={"tim": 1 - half},
            device_id_type=MESH,
        )
        lax.fori_loop((1 - half) * blocks, (2 - half) * blocks, correlate, 0)
        last.start()
        lax.fori_loop(half * blocks, (1 + half) * blocks, correlate, 0)

        def sent(d, carry):
            turn_copy(d).wait_send()
            return carry

        lax.fori_loop(1, stations, sent, 0)

        @pl.when(half == 0)
        def _():
            near.wait_send()

        last.wait()
        normaliser = 1.0 / (per_group * frames * 2)
        out_ref[...] = (products[pl.ds(half * blocks, blocks)] + other[...]) * normaliser


def per_device(samples, taps, flags, group_owner):
    inputs, frames, fft_len = samples.shape
    taps_count = taps.shape[0]
    stations = lax.axis_size("stn")
    band = flags.shape[0]
    per_group = band // stations
    columns = 2 * band
    total_inputs = stations * inputs
    blocks = total_inputs // ROW_BLOCK
    length = frames * 2 * per_group
    width = min(STEP_WIDTH, fft_len)
    steps = fft_len // width
    span = steps
    while span > 1 and span * width * columns * 2 > TABLE_LIMIT:
        span //= 2
    carry_rows = (taps_count - 1) * inputs
    row_count = frames * inputs + carry_rows
    total_shape = (row_count, columns) if span < steps else (8, LANES)
    tables = [jnp.asarray(t) for t in phase_tables(fft_len, stations, per_group)]
    per_step = width // LANES
    whole = lambda j: (0, 0)
    result = pl.pallas_call(
        functools.partial(kernel, (stations, per_group, steps, span)),
        grid=(steps,),
        in_specs=[
            pl.BlockSpec(memory_space=pltpu.SMEM),
            pl.BlockSpec((inputs, frames, width), lambda j: (0, 0, j)),
            pl.BlockSpec((taps_count, width), lambda j: (0, j)),
            pl.BlockSpec((per_step, columns), lambda j: (j, 0)),
            pl.BlockSpec((per_step, columns), lambda j: (j, 0)),
            pl.BlockSpec((LANES, columns), whole),
            pl.BlockSpec((LANES, columns), whole),
            pl.BlockSpec((flags.shape[1], band), whole),
        ],
        out_specs=pl.BlockSpec((blocks // 2, 2, ROW_BLOCK, total_inputs), lambda j: (0, 0, 0, 0)),
        out_shape=jax.ShapeDtypeStruct((blocks // 2, 2, ROW_BLOCK, total_inputs), jnp.float32),
        scratch_shapes=[
            pltpu.VMEM((inputs * frames, LANES), jnp.float32),
            pltpu.VMEM((row_count, span * width), jnp.bfloat16),
            pltpu.VMEM((span * width, columns), jnp.bfloat16),
            pltpu.VMEM(total_shape, jnp.float32),
            pltpu.VMEM((frames, columns), jnp.float32),
            pltpu.VMEM((carry_rows, columns), jnp.float32),
            pltpu.VMEM((carry_rows, columns), jnp.float32),
            pltpu.VMEM((frames * inputs, columns), jnp.bfloat16),
            pltpu.VMEM((stations, inputs, length), jnp.bfloat16),
            pltpu.VMEM((stations, inputs, length), jnp.bfloat16),
            pltpu.VMEM((blocks, 2, ROW_BLOCK, total_inputs), jnp.float32),
            pltpu.VMEM((blocks // 2, 2, ROW_BLOCK, total_inputs), jnp.float32),
            pltpu.SemaphoreType.DMA((2,)),
            pltpu.SemaphoreType.DMA((stations,)),
            pltpu.SemaphoreType.DMA((stations,)),
            pltpu.SemaphoreType.DMA((2,)),
        ],
        compiler_params=pltpu.CompilerParams(
            collective_id=0, has_side_effects=True, vmem_limit_bytes=60 << 20
        ),
        name="correlator",
    )(group_owner, samples, taps, *tables, flags.T)
    return result.transpose(0, 2, 1, 3).reshape(1, -1, 2, total_inputs)


def solution(mesh):
    in_specs = (P(("grp", "stn"), "tim", None), P(), P("grp", None), P("grp"))
    out_specs = P(("grp", "stn"), "tim", None, None)
    return jax.shard_map(
        per_device, mesh=mesh, in_specs=in_specs, out_specs=out_specs, check_vma=False
    )
```

```python
import functools
import math

import jax
import jax.numpy as jnp
import numpy as np
from jax import lax
from jax.experimental import pallas as pl
from jax.experimental.pallas import tpu as pltpu
from jax.sharding import PartitionSpec as P

BAND_START = 1536
MESH = pl.DeviceIdType.MESH
LANES = 128
ROW_BLOCK = 64
STEP_WIDTH = 1024
TABLE_LIMIT = 8 << 20


def phase_tables(fft_len, groups, per_group):
    channels = np.arange(groups * per_group).reshape(groups, per_group) + BAND_START

    def planes(first, second):
        stacked = np.stack([first, second], axis=-2)
        return stacked.reshape(stacked.shape[0], -1).astype(np.float32)

    def angle(positions):
        index = (positions[:, None, None].astype(np.int64) * channels[None]) % fft_len
        return index * (2.0 * math.pi / fft_len)

    outer = angle(np.arange(fft_len // LANES) * LANES)
    inner = angle(np.arange(LANES))
    amplitude = 1.0 / math.sqrt(fft_len)
    outer_same = planes(np.cos(outer), np.cos(outer))
    outer_cross = planes(np.sin(outer), -np.sin(outer))
    inner_own = planes(np.cos(inner) * amplitude, -np.sin(inner) * amplitude)
    inner_swap = planes(-np.sin(inner) * amplitude, np.cos(inner) * amplitude)
    return outer_same, outer_cross, inner_own, inner_swap


def filter_chunk(samples_ref, taps_ref, wide, rows, lanes, to):
    inputs, frames, _ = samples_ref.shape
    taps_count = taps_ref.shape[0]
    wide[...] = samples_ref[:, :, lanes].astype(jnp.float32).reshape(inputs * frames, LANES)
    weights = [
        jnp.broadcast_to(taps_ref[k : k + 1, lanes], (inputs, LANES)).astype(jnp.bfloat16)
        for k in range(taps_count)
    ]
    frame = [wide[pl.ds(s, inputs, stride=frames), :].astype(jnp.bfloat16) for s in range(frames)]
    for t in range(frames + taps_count - 1):
        first = t - (taps_count - 1)
        terms = [weights[k] * frame[first + k] for k in range(taps_count) if 0 <= first + k < frames]
        while len(terms) > 1:
            paired = [terms[m] + terms[m + 1] for m in range(0, len(terms) - 1, 2)]
            terms = paired + (terms[-1:] if len(terms) % 2 else [])
        rows[t * inputs : (t + 1) * inputs, to] = terms[0]


def kernel(
    dims, owner_ref, samples_ref, taps_ref, same_ref, cross_ref, own_ref, swap_ref, flags_ref, out_ref,
    wide, rows, table, total, valid, later, earlier, spectra, outgoing, received, products, other,
    near_sem, send_sem, recv_sem, final_sem,
):
    stations, per_group, steps, span = dims
    inputs, frames, width = samples_ref.shape
    carry_rows = later.shape[0]
    own_rows = frames * inputs
    group_width = 2 * per_group
    columns = stations * group_width
    per_lane = LANES // group_width
    step = pl.program_id(0)
    me = lax.axis_index("stn")
    half = lax.axis_index("tim")
    barrier = pltpu.get_barrier_semaphore()

    @pl.when(step == 0)
    def _():
        pl.semaphore_signal(barrier, inc=1, device_id={"tim": 1 - half}, device_id_type=MESH)

        def greet(d, carry):
            pl.semaphore_signal(
                barrier, inc=1, device_id={"stn": lax.rem(me + d, stations)}, device_id_type=MESH
            )
            return carry

        lax.fori_loop(1, stations, greet, 0)
        if span < steps:
            total[...] = jnp.zeros_like(total)
        band = stations * per_group
        channel = lax.broadcasted_iota(jnp.int32, (band, columns), 0)
        column = lax.broadcasted_iota(jnp.int32, (band, columns), 1)
        spread = (channel == column // group_width * per_group + column % per_group).astype(jnp.bfloat16)
        flag_rows = flags_ref[...].astype(jnp.float32).astype(jnp.bfloat16)
        both = jnp.dot(flag_rows, spread, preferred_element_type=jnp.float32)
        valid[...] = jnp.where(half == 0, both[:frames], both[frames:])

    place = lax.rem(step, span) * width

    def chunks(fill):
        def chunk(c, carry):
            lanes = pl.ds(pl.multiple_of(c * LANES, LANES), LANES)
            filter_chunk(samples_ref, taps_ref, wide, rows, lanes, pl.ds(pl.multiple_of(place + c * LANES, LANES), LANES))
            fill(c, place + c * LANES)
            return carry

        lax.fori_loop(0, width // LANES, chunk, 0, unroll=4)

    def build(c, to):
        table[pl.ds(pl.multiple_of(to, LANES), LANES), :] = (
            same_ref[pl.ds(c, 1), :] * own_ref[...] + cross_ref[pl.ds(c, 1), :] * swap_ref[...]
        ).astype(table.dtype)

    if span == steps and steps % 2 == 0:
        middle = table.shape[0] // 2
        lane_column = lax.broadcasted_iota(jnp.int32, (LANES, columns), 1)
        bins = BAND_START + lane_column // group_width * per_group + lane_column % per_group
        sign = (1 - 2 * (bins % 2)).astype(jnp.float32).astype(table.dtype)

        def mirror(c, to):
            source = table[pl.ds(pl.multiple_of(to - middle, LANES), LANES), :]
            table[pl.ds(pl.multiple_of(to, LANES), LANES), :] = source * sign

        @pl.when(step < steps // 2)
        def _():
            chunks(build)

        @pl.when(step >= steps // 2)
        def _():
            chunks(mirror)
    else:
        chunks(build)

    def transform(low, high):
        return jnp.dot(rows[low:high, :], table[...], preferred_element_type=jnp.float32)

    if span < steps:

        @pl.when(jnp.logical_and(lax.rem(step, span) == span - 1, step < steps - 1))
        def _():
            total[...] += transform(0, own_rows + carry_rows)

    @pl.when(step == steps - 1)
    def _():
        def finished(low, high):
            result = transform(low, high)
            return result + total[low:high, :] if span < steps else result

        later[...] = finished(own_rows, own_rows + carry_rows)
        pl.semaphore_wait(barrier, stations)
        near = pltpu.make_async_remote_copy(
            src_ref=later,
            dst_ref=earlier,
            send_sem=near_sem.at[0],
            recv_sem=near_sem.at[1],
            device_id={"tim": 1 - half},
            device_id_type=MESH,
        )

        @pl.when(half == 0)
        def _():
            near.start()

        mine = finished(0, own_rows)
        lane = lax.broadcasted_iota(jnp.int32, (8, columns), 1)
        target = lane % group_width
        for g in range(stations):
            target = jnp.where(lane // group_width == g, target + owner_ref[g] * group_width, target)
        target = target[:1]
        mask = valid[...].astype(jnp.bfloat16)

        def weigh(values, low, high):
            count = high - low
            shaped = values.astype(jnp.bfloat16).reshape(count, inputs, columns)
            spectra[low * inputs : high * inputs, :] = (shaped * mask[low:high, None, :]).reshape(
                count * inputs, columns
            )

        @pl.when(half == 0)
        def _():
            weigh(mine, 0, frames)

        @pl.when(half == 1)
        def _():
            near.wait_recv()
            carried = carry_rows // inputs
            weigh(mine[:carry_rows] + earlier[...], 0, carried)
            weigh(mine[carry_rows:], carried, frames)

        slot = lax.broadcasted_iota(jnp.int32, (inputs, LANES), 1) // group_width

        def turn_copy(d):
            to = lax.rem(me + d, stations)
            return pltpu.make_async_remote_copy(
                src_ref=outgoing.at[to],
                dst_ref=received.at[me],
                send_sem=send_sem.at[d],
                recv_sem=recv_sem.at[d],
                device_id={"stn": to},
                device_id_type=MESH,
            )

        def arrange(b, carry):
            row = lax.broadcasted_iota(jnp.int32, (LANES, columns), 0) + b * LANES
            picked = (row == target).astype(jnp.bfloat16)
            block = lax.dot_general(
                spectra[...], picked, (((1,), (1,)), ((), ())), preferred_element_type=jnp.float32
            )
            for r in range(per_lane):
                for quad in range(frames // per_lane):
                    joined = jnp.zeros((inputs, LANES), jnp.float32)
                    for t in range(per_lane):
                        first = (quad * per_lane + t) * inputs
                        piece = block[first : first + inputs, :]
                        if t != r:
                            piece = pltpu.roll(piece, ((t - r) * group_width) % LANES, 1)
                        joined = jnp.where(slot == t, piece, joined)
                    outgoing[b * per_lane + r, :, quad * LANES : (quad + 1) * LANES] = joined.astype(
                        jnp.bfloat16
                    )
            return carry

        lax.fori_loop(0, stations // per_lane, arrange, 0)

        def send(d, carry):
            turn_copy(d).start()
            return carry

        lax.fori_loop(1, stations, send, 0)
        received[me] = outgoing[me]

        def arrive(d, carry):
            turn_copy(d).wait_recv()
            return carry

        lax.fori_loop(1, stations, arrive, 0)

        total_inputs = stations * inputs
        length = frames * group_width
        per_block = ROW_BLOCK // inputs
        plane = lax.broadcasted_iota(jnp.int32, (ROW_BLOCK, length), 1) // per_group % 2
        everything = received[...].reshape(total_inputs, length)

        def correlate(b, carry):
            left = received[pl.ds(b * per_block, per_block)].reshape(ROW_BLOCK, length)
            full = left.astype(jnp.float32)
            turned = jnp.where(
                plane == 0, pltpu.roll(full, length - per_group, 1), -pltpu.roll(full, per_group, 1)
            ).astype(jnp.bfloat16)
            pair = jnp.concatenate([left, turned], axis=0)
            product = lax.dot_general(
                pair, everything, (((1,), (1,)), ((), ())), preferred_element_type=jnp.float32
            )
            products[b] = product.reshape(2, ROW_BLOCK, total_inputs)
            return carry

        blocks = out_ref.shape[0]
        last = pltpu.make_async_remote_copy(
            src_ref=products.at[pl.ds((1 - half) * blocks, blocks)],
            dst_ref=other,
            send_sem=final_sem.at[0],
            recv_sem=final_sem.at[1],
            device_id={"tim": 1 - half},
            device_id_type=MESH,
        )
        lax.fori_loop((1 - half) * blocks, (2 - half) * blocks, correlate, 0)
        last.start()
        lax.fori_loop(half * blocks, (1 + half) * blocks, correlate, 0)

        def sent(d, carry):
            turn_copy(d).wait_send()
            return carry

        lax.fori_loop(1, stations, sent, 0)

        @pl.when(half == 0)
        def _():
            near.wait_send()

        last.wait()
        normaliser = 1.0 / (per_group * frames * 2)
        out_ref[...] = (products[pl.ds(half * blocks, blocks)] + other[...]) * normaliser


def per_device(samples, taps, flags, group_owner):
    inputs, frames, fft_len = samples.shape
    taps_count = taps.shape[0]
    stations = lax.axis_size("stn")
    band = flags.shape[0]
    per_group = band // stations
    columns = 2 * band
    total_inputs = stations * inputs
    blocks = total_inputs // ROW_BLOCK
    length = frames * 2 * per_group
    width = min(STEP_WIDTH, fft_len)
    steps = fft_len // width
    span = steps
    while span > 1 and span * width * columns * 2 > TABLE_LIMIT:
        span //= 2
    carry_rows = (taps_count - 1) * inputs
    row_count = frames * inputs + carry_rows
    total_shape = (row_count, columns) if span < steps else (8, LANES)
    tables = [jnp.asarray(t) for t in phase_tables(fft_len, stations, per_group)]
    per_step = width // LANES
    whole = lambda j: (0, 0)
    result = pl.pallas_call(
        functools.partial(kernel, (stations, per_group, steps, span)),
        grid=(steps,),
        in_specs=[
            pl.BlockSpec(memory_space=pltpu.SMEM),
            pl.BlockSpec((inputs, frames, width), lambda j: (0, 0, j)),
            pl.BlockSpec((taps_count, width), lambda j: (0, j)),
            pl.BlockSpec((per_step, columns), lambda j: (j, 0)),
            pl.BlockSpec((per_step, columns), lambda j: (j, 0)),
            pl.BlockSpec((LANES, columns), whole),
            pl.BlockSpec((LANES, columns), whole),
            pl.BlockSpec((flags.shape[1], band), whole),
        ],
        out_specs=pl.BlockSpec((blocks // 2, 2, ROW_BLOCK, total_inputs), lambda j: (0, 0, 0, 0)),
        out_shape=jax.ShapeDtypeStruct((blocks // 2, 2, ROW_BLOCK, total_inputs), jnp.float32),
        scratch_shapes=[
            pltpu.VMEM((inputs * frames, LANES), jnp.float32),
            pltpu.VMEM((row_count, span * width), jnp.bfloat16),
            pltpu.VMEM((span * width, columns), jnp.bfloat16),
            pltpu.VMEM(total_shape, jnp.float32),
            pltpu.VMEM((frames, columns), jnp.float32),
            pltpu.VMEM((carry_rows, columns), jnp.float32),
            pltpu.VMEM((carry_rows, columns), jnp.float32),
            pltpu.VMEM((frames * inputs, columns), jnp.bfloat16),
            pltpu.VMEM((stations, inputs, length), jnp.bfloat16),
            pltpu.VMEM((stations, inputs, length), jnp.bfloat16),
            pltpu.VMEM((blocks, 2, ROW_BLOCK, total_inputs), jnp.float32),
            pltpu.VMEM((blocks // 2, 2, ROW_BLOCK, total_inputs), jnp.float32),
            pltpu.SemaphoreType.DMA((2,)),
            pltpu.SemaphoreType.DMA((stations,)),
            pltpu.SemaphoreType.DMA((stations,)),
            pltpu.SemaphoreType.DMA((2,)),
        ],
        compiler_params=pltpu.CompilerParams(
            collective_id=0, has_side_effects=True, vmem_limit_bytes=60 << 20
        ),
        name="correlator",
    )(group_owner, samples, taps, *tables, flags.T)
    return result.transpose(0, 2, 1, 3).reshape(1, -1, 2, total_inputs)


def solution(mesh):
    in_specs = (P(("grp", "stn"), "tim", None), P(), P("grp", None), P("grp"))
    out_specs = P(("grp", "stn"), "tim", None, None)
    return jax.shard_map(
        per_device, mesh=mesh, in_specs=in_specs, out_specs=out_specs, check_vma=False
    )
```

```python
import functools
import math

import jax
import jax.numpy as jnp
import numpy as np
from jax import lax
from jax.experimental import pallas as pl
from jax.experimental.pallas import tpu as pltpu
from jax.sharding import PartitionSpec as P

BAND_START = 1536
MESH = pl.DeviceIdType.MESH
LANES = 128
ROW_BLOCK = 64
STEP_WIDTH = 1024
TABLE_LIMIT = 8 << 20


def phase_tables(fft_len, groups, per_group):
    channels = np.arange(groups * per_group).reshape(groups, per_group) + BAND_START

    def planes(first, second):
        stacked = np.stack([first, second], axis=-2)
        return stacked.reshape(stacked.shape[0], -1).astype(np.float32)

    def angle(positions):
        index = (positions[:, None, None].astype(np.int64) * channels[None]) % fft_len
        return index * (2.0 * math.pi / fft_len)

    outer = angle(np.arange(fft_len // LANES) * LANES)
    inner = angle(np.arange(LANES))
    amplitude = 1.0 / math.sqrt(fft_len)
    outer_same = planes(np.cos(outer), np.cos(outer))
    outer_cross = planes(np.sin(outer), -np.sin(outer))
    inner_own = planes(np.cos(inner) * amplitude, -np.sin(inner) * amplitude)
    inner_swap = planes(-np.sin(inner) * amplitude, np.cos(inner) * amplitude)
    return outer_same, outer_cross, inner_own, inner_swap


def filter_chunk(samples_ref, taps_ref, wide, rows, lanes, to):
    inputs, frames, _ = samples_ref.shape
    taps_count = taps_ref.shape[0]
    wide[...] = samples_ref[:, :, lanes].astype(jnp.float32).reshape(inputs * frames, LANES)
    weights = [
        jnp.broadcast_to(taps_ref[k : k + 1, lanes], (inputs, LANES)).astype(jnp.bfloat16)
        for k in range(taps_count)
    ]
    frame = [wide[pl.ds(s, inputs, stride=frames), :].astype(jnp.bfloat16) for s in range(frames)]
    for t in range(frames + taps_count - 1):
        first = t - (taps_count - 1)
        terms = [weights[k] * frame[first + k] for k in range(taps_count) if 0 <= first + k < frames]
        while len(terms) > 1:
            paired = [terms[m] + terms[m + 1] for m in range(0, len(terms) - 1, 2)]
            terms = paired + (terms[-1:] if len(terms) % 2 else [])
        rows[t * inputs : (t + 1) * inputs, to] = terms[0]


def kernel(
    dims, owner_ref, samples_ref, taps_ref, same_ref, cross_ref, own_ref, swap_ref, flags_ref, out_ref,
    wide, rows, table, total, valid, later, earlier, spectra, outgoing, received, products, other,
    near_sem, send_sem, recv_sem, final_sem,
):
    stations, per_group, steps, span = dims
    inputs, frames, width = samples_ref.shape
    carry_rows = later.shape[0]
    own_rows = frames * inputs
    group_width = 2 * per_group
    columns = stations * group_width
    per_lane = LANES // group_width
    step = pl.program_id(0)
    me = lax.axis_index("stn")
    half = lax.axis_index("tim")
    barrier = pltpu.get_barrier_semaphore()

    @pl.when(step == 0)
    def _():
        pl.semaphore_signal(barrier, inc=1, device_id={"tim": 1 - half}, device_id_type=MESH)

        def greet(d, carry):
            pl.semaphore_signal(
                barrier, inc=1, device_id={"stn": lax.rem(me + d, stations)}, device_id_type=MESH
            )
            return carry

        lax.fori_loop(1, stations, greet, 0)
        if span < steps:
            total[...] = jnp.zeros_like(total)
        band = stations * per_group
        channel = lax.broadcasted_iota(jnp.int32, (band, columns), 0)
        column = lax.broadcasted_iota(jnp.int32, (band, columns), 1)
        spread = (channel == column // group_width * per_group + column % per_group).astype(jnp.bfloat16)
        flag_rows = flags_ref[...].astype(jnp.float32).astype(jnp.bfloat16)
        both = jnp.dot(flag_rows, spread, preferred_element_type=jnp.float32)
        valid[...] = jnp.where(half == 0, both[:frames], both[frames:])

    place = lax.rem(step, span) * width

    def chunks(fill):
        def chunk(c, carry):
            lanes = pl.ds(pl.multiple_of(c * LANES, LANES), LANES)
            filter_chunk(samples_ref, taps_ref, wide, rows, lanes, pl.ds(pl.multiple_of(place + c * LANES, LANES), LANES))
            fill(c, place + c * LANES)
            return carry

        lax.fori_loop(0, width // LANES, chunk, 0, unroll=4)

    def build(c, to):
        table[pl.ds(pl.multiple_of(to, LANES), LANES), :] = (
            same_ref[pl.ds(c, 1), :] * own_ref[...] + cross_ref[pl.ds(c, 1), :] * swap_ref[...]
        ).astype(table.dtype)

    if span == steps and steps % 2 == 0:
        middle = table.shape[0] // 2
        lane_column = lax.broadcasted_iota(jnp.int32, (LANES, columns), 1)
        bins = BAND_START + lane_column // group_width * per_group + lane_column % per_group
        sign = (1 - 2 * (bins % 2)).astype(jnp.float32).astype(table.dtype)

        def mirror(c, to):
            source = table[pl.ds(pl.multiple_of(to - middle, LANES), LANES), :]
            table[pl.ds(pl.multiple_of(to, LANES), LANES), :] = source * sign

        @pl.when(step < steps // 2)
        def _():
            chunks(build)

        @pl.when(step >= steps // 2)
        def _():
            chunks(mirror)
    else:
        chunks(build)

    def transform(low, high):
        return jnp.dot(rows[low:high, :], table[...], preferred_element_type=jnp.float32)

    if span < steps:

        @pl.when(jnp.logical_and(lax.rem(step, span) == span - 1, step < steps - 1))
        def _():
            total[...] += transform(0, own_rows + carry_rows)

    @pl.when(step == steps - 1)
    def _():
        def finished(low, high):
            result = transform(low, high)
            return result + total[low:high, :] if span < steps else result

        later[...] = finished(own_rows, own_rows + carry_rows)
        pl.semaphore_wait(barrier, stations)
        near = pltpu.make_async_remote_copy(
            src_ref=later,
            dst_ref=earlier,
            send_sem=near_sem.at[0],
            recv_sem=near_sem.at[1],
            device_id={"tim": 1 - half},
            device_id_type=MESH,
        )

        @pl.when(half == 0)
        def _():
            near.start()

        mine = finished(0, own_rows)
        lane = lax.broadcasted_iota(jnp.int32, (8, columns), 1)
        target = lane % group_width
        for g in range(stations):
            target = jnp.where(lane // group_width == g, target + owner_ref[g] * group_width, target)
        target = target[:1]
        mask = valid[...].astype(jnp.bfloat16)

        def weigh(values, low, high):
            count = high - low
            shaped = values.astype(jnp.bfloat16).reshape(count, inputs, columns)
            spectra[low * inputs : high * inputs, :] = (shaped * mask[low:high, None, :]).reshape(
                count * inputs, columns
            )

        @pl.when(half == 0)
        def _():
            weigh(mine, 0, frames)

        @pl.when(half == 1)
        def _():
            near.wait_recv()
            carried = carry_rows // inputs
            weigh(mine[:carry_rows] + earlier[...], 0, carried)
            weigh(mine[carry_rows:], carried, frames)

        slot = lax.broadcasted_iota(jnp.int32, (inputs, LANES), 1) // group_width

        def turn_copy(d):
            to = lax.rem(me + d, stations)
            return pltpu.make_async_remote_copy(
                src_ref=outgoing.at[to],
                dst_ref=received.at[me],
                send_sem=send_sem.at[d],
                recv_sem=recv_sem.at[d],
                device_id={"stn": to},
                device_id_type=MESH,
            )

        def arrange(turn, carry):
            b = lax.rem(turn + 1 + me // per_lane, stations // per_lane)
            row = lax.broadcasted_iota(jnp.int32, (LANES, columns), 0) + b * LANES
            picked = (row == target).astype(jnp.bfloat16)
            block = lax.dot_general(
                spectra[...], picked, (((1,), (1,)), ((), ())), preferred_element_type=jnp.float32
            )
            for r in range(per_lane):
                for quad in range(frames // per_lane):
                    joined = jnp.zeros((inputs, LANES), jnp.float32)
                    for t in range(per_lane):
                        first = (quad * per_lane + t) * inputs
                        piece = block[first : first + inputs, :]
                        if t != r:
                            piece = pltpu.roll(piece, ((t - r) * group_width) % LANES, 1)
                        joined = jnp.where(slot == t, piece, joined)
                    outgoing[b * per_lane + r, :, quad * LANES : (quad + 1) * LANES] = joined.astype(
                        jnp.bfloat16
                    )
            for r in range(per_lane):
                to = b * per_lane + r

                @pl.when(to != me)
                def _():
                    turn_copy(lax.rem(to - me + stations, stations)).start()

            return carry

        lax.fori_loop(0, stations // per_lane, arrange, 0)

        received[me] = outgoing[me]

        def arrive(d, carry):
            turn_copy(d).wait_recv()
            return carry

        lax.fori_loop(1, stations, arrive, 0)

        total_inputs = stations * inputs
        length = frames * group_width
        per_block = ROW_BLOCK // inputs
        plane = lax.broadcasted_iota(jnp.int32, (ROW_BLOCK, length), 1) // per_group % 2
        everything = received[...].reshape(total_inputs, length)

        def correlate(b, carry):
            left = received[pl.ds(b * per_block, per_block)].reshape(ROW_BLOCK, length)
            full = left.astype(jnp.float32)
            turned = jnp.where(
                plane == 0, pltpu.roll(full, length - per_group, 1), -pltpu.roll(full, per_group, 1)
            ).astype(jnp.bfloat16)
            pair = jnp.concatenate([left, turned], axis=0)
            product = lax.dot_general(
                pair, everything, (((1,), (1,)), ((), ())), preferred_element_type=jnp.float32
            )
            products[b] = product.reshape(2, ROW_BLOCK, total_inputs)
            return carry

        blocks = out_ref.shape[0]
        last = pltpu.make_async_remote_copy(
            src_ref=products.at[pl.ds((1 - half) * blocks, blocks)],
            dst_ref=other,
            send_sem=final_sem.at[0],
            recv_sem=final_sem.at[1],
            device_id={"tim": 1 - half},
            device_id_type=MESH,
        )
        lax.fori_loop((1 - half) * blocks, (2 - half) * blocks, correlate, 0)
        last.start()
        lax.fori_loop(half * blocks, (1 + half) * blocks, correlate, 0)

        def sent(d, carry):
            turn_copy(d).wait_send()
            return carry

        lax.fori_loop(1, stations, sent, 0)

        @pl.when(half == 0)
        def _():
            near.wait_send()

        last.wait()
        normaliser = 1.0 / (per_group * frames * 2)
        out_ref[...] = (products[pl.ds(half * blocks, blocks)] + other[...]) * normaliser


def per_device(samples, taps, flags, group_owner):
    inputs, frames, fft_len = samples.shape
    taps_count = taps.shape[0]
    stations = lax.axis_size("stn")
    band = flags.shape[0]
    per_group = band // stations
    columns = 2 * band
    total_inputs = stations * inputs
    blocks = total_inputs // ROW_BLOCK
    length = frames * 2 * per_group
    width = min(STEP_WIDTH, fft_len)
    steps = fft_len // width
    span = steps
    while span > 1 and span * width * columns * 2 > TABLE_LIMIT:
        span //= 2
    carry_rows = (taps_count - 1) * inputs
    row_count = frames * inputs + carry_rows
    total_shape = (row_count, columns) if span < steps else (8, LANES)
    tables = [jnp.asarray(t) for t in phase_tables(fft_len, stations, per_group)]
    per_step = width // LANES
    whole = lambda j: (0, 0)
    result = pl.pallas_call(
        functools.partial(kernel, (stations, per_group, steps, span)),
        grid=(steps,),
        in_specs=[
            pl.BlockSpec(memory_space=pltpu.SMEM),
            pl.BlockSpec((inputs, frames, width), lambda j: (0, 0, j)),
            pl.BlockSpec((taps_count, width), lambda j: (0, j)),
            pl.BlockSpec((per_step, columns), lambda j: (j, 0)),
            pl.BlockSpec((per_step, columns), lambda j: (j, 0)),
            pl.BlockSpec((LANES, columns), whole),
            pl.BlockSpec((LANES, columns), whole),
            pl.BlockSpec((flags.shape[1], band), whole),
        ],
        out_specs=pl.BlockSpec((blocks // 2, 2, ROW_BLOCK, total_inputs), lambda j: (0, 0, 0, 0)),
        out_shape=jax.ShapeDtypeStruct((blocks // 2, 2, ROW_BLOCK, total_inputs), jnp.float32),
        scratch_shapes=[
            pltpu.VMEM((inputs * frames, LANES), jnp.float32),
            pltpu.VMEM((row_count, span * width), jnp.bfloat16),
            pltpu.VMEM((span * width, columns), jnp.bfloat16),
            pltpu.VMEM(total_shape, jnp.float32),
            pltpu.VMEM((frames, columns), jnp.float32),
            pltpu.VMEM((carry_rows, columns), jnp.float32),
            pltpu.VMEM((carry_rows, columns), jnp.float32),
            pltpu.VMEM((frames * inputs, columns), jnp.bfloat16),
            pltpu.VMEM((stations, inputs, length), jnp.bfloat16),
            pltpu.VMEM((stations, inputs, length), jnp.bfloat16),
            pltpu.VMEM((blocks, 2, ROW_BLOCK, total_inputs), jnp.float32),
            pltpu.VMEM((blocks // 2, 2, ROW_BLOCK, total_inputs), jnp.float32),
            pltpu.SemaphoreType.DMA((2,)),
            pltpu.SemaphoreType.DMA((stations,)),
            pltpu.SemaphoreType.DMA((stations,)),
            pltpu.SemaphoreType.DMA((2,)),
        ],
        compiler_params=pltpu.CompilerParams(
            collective_id=0, has_side_effects=True, vmem_limit_bytes=60 << 20
        ),
        name="correlator",
    )(group_owner, samples, taps, *tables, flags.T)
    return result.transpose(0, 2, 1, 3).reshape(1, -1, 2, total_inputs)


def solution(mesh):
    in_specs = (P(("grp", "stn"), "tim", None), P(), P("grp", None), P("grp"))
    out_specs = P(("grp", "stn"), "tim", None, None)
    return jax.shard_map(
        per_device, mesh=mesh, in_specs=in_specs, out_specs=out_specs, check_vma=False
    )
```
